32 devices in a mesh: rows: 2 (over y), dp: 16 (over z, x, core).
Axes of the slice: x: 2, y: 2, z: 4, core: 2. Of those that a mesh axis runs over, the one named last changes fastest.
Arguments:
- images: bfloat16 [48, 14, 14, 512], P('dp', 'rows'), may hold values from -6 to 6
- cotangent: bfloat16 [48, 14, 14, 512], P('dp', 'rows'), may hold values from -6 to 6
- attn_in_weight: bfloat16 [2, 512, 1536], P(None, 'dp'), may hold values from -0.25 to 0.25
- attn_out_weight: bfloat16 [2, 512, 512], P(None, 'dp'), may hold values from -0.75 to 0.75
- mlp_in_weight: bfloat16 [2, 512, 2048], P(None, 'dp'), may hold values from -0.25 to 0.25
- mlp_out_weight: bfloat16 [2, 2048, 512], P(None, 'dp'), may hold values from -0.125 to 0.125
- norm1_gain: bfloat16 [2, 512], P(None, 'dp'), may hold values from 0.5 to 1.5
- norm1_bias: bfloat16 [2, 512], P(None, 'dp'), may hold values from -1.5 to 1.5
- attn_in_bias: bfloat16 [2, 1024], P(None, 'dp'), may hold values from -1.5 to 1.5
- attn_out_bias: bfloat16 [2, 512], P(None, 'dp'), may hold values from -1.5 to 1.5
- norm2_gain: bfloat16 [2, 512], P(None, 'dp'), may hold values from 0.5 to 1.5
- norm2_bias: bfloat16 [2, 512], P(None, 'dp'), may hold values from -1.5 to 1.5
- mlp_in_bias: bfloat16 [2, 2048], P(None, 'dp'), may hold values from -1.5 to 1.5
- mlp_out_bias: bfloat16 [2, 512], P(None, 'dp'), may hold values from -1.5 to 1.5
- bias_table: float32 [2, 169, 16], replicated, may hold values from -5 to 303
- region_labels: int32 [14, 14], replicated, may hold values from 0 to 2
- table_index: int32 [49, 49], replicated, may hold values from 0 to 168
Outputs:
- final_out: bfloat16 [48, 14, 14, 512], P('dp', 'rows')
- input_grad: float32 [48, 14, 14, 512], P('dp', 'rows')
- grad_attn_in_weight: float32 [2, 512, 1536], P(None, 'dp')
- grad_attn_out_weight: float32 [2, 512, 512], P(None, 'dp')
- grad_mlp_in_weight: float32 [2, 512, 2048], P(None, 'dp')
- grad_mlp_out_weight: float32 [2, 2048, 512], P(None, 'dp')
- grad_norm1_gain: float32 [2, 512], P(None, 'dp')
- grad_norm1_bias: float32 [2, 512], P(None, 'dp')
- grad_attn_in_bias: float32 [2, 1024], P(None, 'dp')
- grad_attn_out_bias: float32 [2, 512], P(None, 'dp')
- grad_norm2_gain: float32 [2, 512], P(None, 'dp')
- grad_norm2_bias: float32 [2, 512], P(None, 'dp')
- grad_mlp_in_bias: float32 [2, 2048], P(None, 'dp')
- grad_mlp_out_bias: float32 [2, 512], P(None, 'dp')
- grad_bias_table: float32 [2, 169, 16], replicated
The draws below stay inside these ranges and needn't reach their ends.
All inputs are finite; a program needn't handle non-finite values.
Results may differ from the reference program's by a relative error of at most 0.015.
Values may be sent and summed in bfloat16 or wider, within the bound.
A program may use at most 192 MiB of HBM per device.

```python
import jax
import jax.numpy as jnp
from jax import lax

C = 512
HEADS = 16
HEAD_DIM = 32
FF = 2048
WIN = 7
GRID = 14
SHIFT = 3
LAYERS = 2
IMG_DEV = 3
IMAGES = 48
REL = 169


def draw_bias_table(key, part):
    shape = (LAYERS, REL, HEADS)
    normal_part = jax.random.truncated_normal(jax.random.fold_in(key, 11), -2.5, 2.5, shape, jnp.float32) * 2.0
    return normal_part


def set_ends(entries, own_key, least, high):
    extent = entries.shape
    spot = [jax.random.randint(jax.random.fold_in(own_key, axis), (), 0, extent[axis]) for axis in range(len(extent))]
    entries = entries.at[tuple(spot)].set(least)
    longest = extent.index(max(extent))
    spot[longest] = (spot[longest] + 1) % extent[longest]
    return entries.at[tuple(spot)].set(high)


def levels(key, shape, cuts, low, top_value):
    def one(dim, shards_of):
        draws = jax.random.uniform(jax.random.fold_in(jax.random.fold_in(key, 6), dim), (shards_of,), jnp.float32, low / len(cuts), top_value / len(cuts))
        return jnp.repeat(jnp.exp(draws), shape[dim] // shards_of).reshape((-1,) + (1,) * (len(shape) - dim - 1))

    level = one(*cuts[0])
    for cut in cuts[1:]:
        level = level * one(*cut)
    return level


def centred(stream_key, dims, scale, limit, pieces=(), kind=jnp.bfloat16):
    entries = jax.random.normal(stream_key, dims, jnp.float32) * scale
    if len(pieces) > 0:
        entries = levels(stream_key, dims, pieces, -0.22, 0.18) * entries
    return jnp.clip(entries, min=-limit, max=limit).astype(kind)


def setup_inputs(seed: int = 0) -> dict:
    key_of = jax.random.split(jax.random.key(seed), 18)
    images = centred(key_of[0], (IMAGES, GRID, GRID, C), 1.0, 6.0, ((0, 16), (1, 2)))
    cotangent = centred(key_of[1], (IMAGES, GRID, GRID, C), 1.0, 6.0, ((0, 16), (1, 2)))
    attn_in_weight = centred(key_of[2], (LAYERS, C, 3 * C), C ** -0.5, 0.25, ((1, 16),))
    attn_out_weight = centred(key_of[3], (LAYERS, C, C), (C // 8) ** -0.5, 0.75, ((1, 16),))
    mlp_in_weight = centred(key_of[4], (LAYERS, C, FF), C ** -0.5, 0.25, ((1, 16),))
    mlp_out_weight = centred(key_of[5], (LAYERS, FF, C), FF ** -0.5, 0.125, ((1, 16),))
    norm1_gain = jnp.clip(1.0 + 0.1 * jax.random.normal(key_of[6], (LAYERS, C), jnp.float32), 0.5, 1.5).astype(jnp.bfloat16)
    norm1_bias = centred(key_of[7], (LAYERS, C), 0.3, 1.5, ((1, 16),))
    attn_in_bias = centred(key_of[8], (LAYERS, 2 * C), 0.3, 1.5, ((1, 16),))
    attn_out_bias = centred(key_of[9], (LAYERS, C), 0.3, 1.5, ((1, 16),))
    norm2_gain = jnp.clip(1.0 + 0.1 * jax.random.normal(key_of[10], (LAYERS, C), jnp.float32), 0.5, 1.5).astype(jnp.bfloat16)
    norm2_bias = centred(key_of[11], (LAYERS, C), 0.3, 1.5, ((1, 16),))
    mlp_in_bias = centred(key_of[12], (LAYERS, FF), 0.3, 1.5, ((1, 16),))
    mlp_out_bias = centred(key_of[13], (LAYERS, C), 0.3, 1.5, ((1, 16),))
    bias_table = draw_bias_table(jax.random.fold_in(key_of[17], 71), 0)
    region_labels = set_ends(jax.random.randint(key_of[15], (GRID, GRID), 0, 3), jax.random.fold_in(key_of[15], 1), 0, 2).astype(jnp.int32)
    table_index = set_ends(jax.random.randint(key_of[16], (WIN * WIN, WIN * WIN), 0, REL), jax.random.fold_in(key_of[16], 1), 0, REL - 1).astype(jnp.int32)
    return {"images": images, "cotangent": cotangent, "attn_in_weight": attn_in_weight, "attn_out_weight": attn_out_weight, "mlp_in_weight": mlp_in_weight, "mlp_out_weight": mlp_out_weight, "norm1_gain": norm1_gain, "norm1_bias": norm1_bias, "attn_in_bias": attn_in_bias, "attn_out_bias": attn_out_bias, "norm2_gain": norm2_gain, "norm2_bias": norm2_bias, "mlp_in_bias": mlp_in_bias, "mlp_out_bias": mlp_out_bias, "bias_table": bias_table, "region_labels": region_labels, "table_index": table_index}


EPS = 1e-05
NEG = -1e+30
SQRT_HALF = 0.7071067811865476
INV_ROOT_TAU = 0.3989422804014327

def product(spec, left, right):
    return jnp.einsum(spec, left.astype(jnp.float32), right.astype(jnp.float32))

def outer(left, right):
    left_flat = left.reshape(-1, left.shape[-1])
    right_flat = right.reshape(-1, right.shape[-1])
    return jnp.dot(left_flat.T, right_flat, preferred_element_type=jnp.float32)

def back_product(grad_rows, weight):
    return jnp.dot(grad_rows, weight.T, preferred_element_type=jnp.float32)

def token_total(values):
    return lax.optimization_barrier(jnp.sum(values.reshape(-1, values.shape[-1]), axis=0))

def to_windows(grid):
    num_images, grid_rows, grid_cols, channels = grid.shape
    split = grid.reshape(num_images, grid_rows // WIN, WIN, grid_cols // WIN, WIN, channels)
    return split.transpose(0, 1, 3, 2, 4, 5).reshape(num_images, grid_rows // WIN * (grid_cols // WIN), WIN * WIN, channels)

def from_windows(window_rows, grid_rows, grid_cols):
    num_images = window_rows.shape[0]
    channels = window_rows.shape[-1]
    split = window_rows.reshape(num_images, grid_rows // WIN, grid_cols // WIN, WIN, WIN, channels)
    return split.transpose(0, 1, 3, 2, 4, 5).reshape(num_images, grid_rows, grid_cols, channels)

def layernorm_apply(values, gain_vector, offset_vector):
    average = lax.optimization_barrier(jnp.mean(values, axis=-1, keepdims=True))
    centered_input = values - average
    variance = lax.optimization_barrier(jnp.mean(centered_input * centered_input, axis=-1, keepdims=True))
    inverse_deviation = lax.rsqrt(variance + EPS)
    standardized = centered_input * inverse_deviation
    return (standardized * gain_vector + offset_vector, standardized, inverse_deviation)

def layernorm_reverse(output_gradient, standardized, inverse_deviation, gain_vector):
    standardized_gradient = output_gradient * gain_vector
    input_gradient_rows = inverse_deviation * (standardized_gradient - lax.optimization_barrier(jnp.mean(standardized_gradient, axis=-1, keepdims=True)) - standardized * lax.optimization_barrier(jnp.mean(standardized_gradient * standardized, axis=-1, keepdims=True)))
    return (input_gradient_rows, token_total(output_gradient * standardized), token_total(output_gradient))

def gelu_value(preactivation):
    return preactivation * 0.5 * (1.0 + lax.erf(preactivation * SQRT_HALF))

def gelu_slope(preactivation):
    return 0.5 * (1.0 + lax.erf(preactivation * SQRT_HALF)) + preactivation * jnp.exp(-0.5 * preactivation * preactivation) * INV_ROOT_TAU

def split_heads(rows):
    return rows.reshape(rows.shape[:-1] + (HEADS, HEAD_DIM))

def masked_scores(window_queries, window_keys, pos_bias, allowed):
    scores = product('bwqhd,bwkhd->bwhqk', split_heads(window_queries), split_heads(window_keys)) + pos_bias[None, None]
    return jnp.where(allowed[None, :, None], scores, NEG)

def attend(window_queries, window_keys, window_values, pos_bias, allowed):
    scores = masked_scores(window_queries, window_keys, pos_bias, allowed)
    row_max = lax.optimization_barrier(jnp.max(scores, axis=-1, keepdims=True))
    log_partition = row_max + jnp.log(lax.optimization_barrier(jnp.sum(jnp.exp(scores - row_max), axis=-1, keepdims=True)))
    attn_probs = jnp.exp(scores - log_partition).astype(jnp.bfloat16)
    context = product('bwhqk,bwkhd->bwqhd', attn_probs, split_heads(window_values))
    return (context.reshape(window_queries.shape).astype(jnp.bfloat16), log_partition)

def attend_back(window_queries, window_keys, window_values, pos_bias, allowed, log_partition, grad_context):
    scores = masked_scores(window_queries, window_keys, pos_bias, allowed)
    attn_probs = jnp.exp(scores - log_partition)
    grad_heads = split_heads(grad_context)
    grad_probs = product('bwqhd,bwkhd->bwhqk', grad_heads, split_heads(window_values))
    grad_values = product('bwhqk,bwqhd->bwkhd', attn_probs.astype(jnp.bfloat16), grad_heads)
    grad_scores = attn_probs * (grad_probs - lax.optimization_barrier(jnp.sum(attn_probs * grad_probs, axis=-1, keepdims=True)))
    table_term = lax.optimization_barrier(jnp.sum(grad_scores, axis=(0, 1)))
    scores_bf = grad_scores.astype(jnp.bfloat16)
    grad_query = product('bwhqk,bwkhd->bwqhd', scores_bf, split_heads(window_keys))
    grad_keys = product('bwhqk,bwqhd->bwkhd', scores_bf, split_heads(window_queries))
    shape = window_queries.shape
    return (grad_query.reshape(shape), grad_keys.reshape(shape), grad_values.reshape(shape), table_term)

def lookup(table_part, table_index):
    picked = jnp.take(table_part, table_index.reshape(-1), axis=0)
    return picked.T.reshape(HEADS, WIN * WIN, WIN * WIN)

def layer_forward(residual_tokens, params, table_part, table_index, allowed, shifted):
    in_weight, out_weight, up_weight, down_weight, first_gain, first_offset, in_bias, out_bias, second_gain, second_offset, up_bias, down_bias = params
    normalized_tokens, first_standardized, first_scale = layernorm_apply(residual_tokens, first_gain, first_offset)
    normalized_tokens = normalized_tokens.astype(jnp.bfloat16)
    if shifted:
        normalized_tokens = jnp.roll(normalized_tokens, (-SHIFT, -SHIFT), axis=(1, 2))
    window_input = to_windows(normalized_tokens)
    packed = jnp.dot(window_input, in_weight, preferred_element_type=jnp.float32)
    window_queries = ((packed[..., :C] + in_bias[:C]) * HEAD_DIM ** (-0.5)).astype(jnp.bfloat16)
    window_keys = packed[..., C:2 * C].astype(jnp.bfloat16)
    window_values = (packed[..., 2 * C:] + in_bias[C:]).astype(jnp.bfloat16)
    pos_bias = lookup(table_part, table_index)
    context, log_partition = attend(window_queries, window_keys, window_values, pos_bias, allowed)
    local_context = from_windows(context, GRID, GRID)
    if shifted:
        local_context = jnp.roll(local_context, (SHIFT, SHIFT), axis=(1, 2))
    attended_residual = residual_tokens + jnp.dot(local_context, out_weight, preferred_element_type=jnp.float32) + out_bias
    second_normalized, second_standardized, second_scale = layernorm_apply(attended_residual, second_gain, second_offset)
    hidden_units = second_normalized.astype(jnp.bfloat16)
    preactivation = jnp.dot(hidden_units, up_weight, preferred_element_type=jnp.float32) + up_bias
    activated_units = gelu_value(preactivation).astype(jnp.bfloat16)
    result = attended_residual + jnp.dot(activated_units, down_weight, preferred_element_type=jnp.float32) + down_bias
    retained_state = (first_standardized, first_scale, window_input, window_queries, window_keys, window_values, log_partition, local_context, second_standardized, second_scale, hidden_units, preactivation, activated_units)
    return (result, retained_state)

def layer_backward(grad_flow, params, table_part, table_index, allowed, onehot, shifted, retained_state):
    in_weight, out_weight, up_weight, down_weight, first_gain, first_offset, in_bias, out_bias, second_gain, second_offset, up_bias, down_bias = params
    first_standardized, first_scale, window_input, window_queries, window_keys, window_values, log_partition, local_context, second_standardized, second_scale, hidden_units, preactivation, activated_units = retained_state
    grad_bf = grad_flow.astype(jnp.bfloat16)
    grad_down = outer(activated_units, grad_bf)
    grad_down_bias = token_total(grad_flow)
    grad_active = back_product(grad_bf, down_weight)
    grad_pre = grad_active * gelu_slope(preactivation)
    grad_pre_bf = grad_pre.astype(jnp.bfloat16)
    grad_upw = outer(hidden_units, grad_pre_bf)
    grad_up_bias = token_total(grad_pre)
    hidden_gradient = back_product(grad_pre_bf, up_weight)
    attention_share, second_gain_gradient, second_offset_gradient = layernorm_reverse(hidden_gradient, second_standardized, second_scale, second_gain)
    grad_mixed = grad_flow + attention_share
    mixed_bf = grad_mixed.astype(jnp.bfloat16)
    grad_outw = outer(local_context, mixed_bf)
    grad_out_bias = token_total(grad_mixed)
    grad_context = back_product(mixed_bf, out_weight).astype(jnp.bfloat16)
    if shifted:
        grad_context = jnp.roll(grad_context, (-SHIFT, -SHIFT), axis=(1, 2))
    grad_context_win = to_windows(grad_context)
    pos_bias = lookup(table_part, table_index)
    grad_query, grad_keys, grad_values, table_term = attend_back(window_queries, window_keys, window_values, pos_bias, allowed, log_partition, grad_context_win)
    grad_query = grad_query * HEAD_DIM ** (-0.5)
    grad_packed = jnp.concatenate([grad_query, grad_keys, grad_values], axis=-1).astype(jnp.bfloat16)
    grad_inw = outer(window_input, grad_packed)
    grad_in_bias = jnp.concatenate([token_total(grad_query), token_total(grad_values)])
    normalized_gradient = from_windows(back_product(grad_packed, in_weight), GRID, GRID)
    if shifted:
        normalized_gradient = jnp.roll(normalized_gradient, (SHIFT, SHIFT), axis=(1, 2))
    residual_share, first_gain_gradient, first_offset_gradient = layernorm_reverse(normalized_gradient, first_standardized, first_scale, first_gain)
    grad_stream = grad_mixed + residual_share
    grad_table = lax.dot_general(onehot, table_term.reshape(HEADS, -1), (((0,), (1,)), ((), ())), precision=lax.Precision.HIGHEST)
    grads = (grad_inw, grad_outw, grad_upw, grad_down, first_gain_gradient, first_offset_gradient, grad_in_bias, grad_out_bias, second_gain_gradient, second_offset_gradient, grad_up_bias, grad_down_bias)
    return (grad_stream, grads, grad_table)

def layer_params(weights, layer_no):
    return tuple((member[layer_no] if position < 4 else member[layer_no].astype(jnp.float32) for position, member in enumerate(weights)))

def two_layers(image_part, cot_part, weights, bias_table, table_index, allowed_pair, onehot):
    residual_tokens = image_part.astype(jnp.float32)
    saved_all = []
    for layer_no in range(LAYERS):
        params = layer_params(weights, layer_no)
        residual_tokens, retained_state = layer_forward(residual_tokens, params, bias_table[layer_no], table_index, allowed_pair[layer_no % 2], layer_no % 2 == 1)
        saved_all.append(retained_state)
    final_out = residual_tokens.astype(jnp.bfloat16)
    grad_flow = cot_part.astype(jnp.float32)
    grads_all = [None] * LAYERS
    tables_all = [None] * LAYERS
    for layer_no in reversed(range(LAYERS)):
        params = layer_params(weights, layer_no)
        grad_flow, grads_all[layer_no], tables_all[layer_no] = layer_backward(grad_flow, params, bias_table[layer_no], table_index, allowed_pair[layer_no % 2], onehot, layer_no % 2 == 1, saved_all[layer_no])
    return (final_out, grad_flow, grads_all, tables_all)

def reference(images, cotangent, attn_in_weight, attn_out_weight, mlp_in_weight, mlp_out_weight, norm1_gain, norm1_bias, attn_in_bias, attn_out_bias, norm2_gain, norm2_bias, mlp_in_bias, mlp_out_bias, bias_table, region_labels, table_index):
    weights = (attn_in_weight, attn_out_weight, mlp_in_weight, mlp_out_weight, norm1_gain, norm1_bias, attn_in_bias, attn_out_bias, norm2_gain, norm2_bias, mlp_in_bias, mlp_out_bias)
    label_tiles = to_windows(region_labels[None, :, :, None])[0, :, :, 0]
    shifted_allowed = label_tiles[:, :, None] == label_tiles[:, None, :]
    allowed_pair = (jnp.ones_like(shifted_allowed), shifted_allowed)
    onehot = (table_index.reshape(-1)[:, None] == jnp.arange(REL, dtype=jnp.int32)[None, :]).astype(jnp.float32)
    block_count = IMAGES // IMG_DEV
    image_blocks = images.reshape(block_count, IMG_DEV, GRID, GRID, C)
    cot_blocks = cotangent.reshape(block_count, IMG_DEV, GRID, GRID, C)
    zero_grads = tuple((jnp.zeros(member.shape, jnp.float32) for member in weights))
    zero_table = jnp.zeros(bias_table.shape, jnp.float32)

    def run_block(carry, inputs):
        grad_sums, table_total = carry
        image_part, cot_part = inputs
        final_out, grad_flow, grads_all, tables_all = two_layers(image_part, cot_part, weights, bias_table, table_index, allowed_pair, onehot)
        new_sums = tuple((grad_sums[position] + jnp.stack([grads_all[layer_no][position] for layer_no in range(LAYERS)]) for position in range(12)))
        return ((new_sums, table_total + jnp.stack(tables_all)), (final_out, grad_flow))
    (grad_sums, table_total), (finals, flows) = lax.scan(run_block, (zero_grads, zero_table), (image_blocks, cot_blocks))
    final_out = finals.reshape(IMAGES, GRID, GRID, C)
    input_grad = flows.reshape(IMAGES, GRID, GRID, C)
    return (final_out, input_grad, grad_sums[0], grad_sums[1], grad_sums[2], grad_sums[3], grad_sums[4], grad_sums[5], grad_sums[6], grad_sums[7], grad_sums[8], grad_sums[9], grad_sums[10], grad_sums[11], table_total)
```

```python
import jax
import jax.numpy as jnp
from jax import lax
from jax.experimental import pallas as pl
from jax.experimental.pallas import tpu as pltpu
from jax.sharding import PartitionSpec as P

C = 512
HEADS = 16
HEAD_DIM = 32
WIN = 7
GRID = 14
SHIFT = 3
LAYERS = 2
REL = 169
SIDE = 8
PAD = SIDE * SIDE
LANES = 128
GROUP = LANES // HEAD_DIM
GROUPS = HEADS // GROUP


EPS = 1e-05
NEG = -1e30
SQRT_HALF = 0.7071067811865476
INV_ROOT_TAU = 0.3989422804014327


def swapped(array, axis, distance):
    return lax.ppermute(array, axis, [(i, i ^ 1 << distance) for i in range(lax.axis_size(axis))])


def product(spec, left, right):
    return jnp.einsum(spec, left, right, preferred_element_type=jnp.float32)


def outer(left, right):
    left_flat = left.reshape(-1, left.shape[-1])
    right_flat = right.reshape(-1, right.shape[-1])
    return lax.dot_general(
        left_flat, right_flat, (((0,), (0,)), ((), ())), preferred_element_type=jnp.float32
    )


def back_product(grad_rows, weight):
    return lax.dot_general(
        grad_rows,
        weight,
        (((grad_rows.ndim - 1,), (1,)), ((), ())),
        preferred_element_type=jnp.float32,
    )


def token_total(values):
    return jnp.sum(values.reshape(-1, values.shape[-1]), axis=0)


def to_padded(grid):
    images, _, cols, channels = grid.shape
    split = grid.reshape(images, WIN, cols // WIN, WIN, channels).transpose(0, 2, 1, 3, 4)
    padded = jnp.pad(split, ((0, 0), (0, 0), (0, SIDE - WIN), (0, SIDE - WIN), (0, 0)))
    return padded.reshape(-1, channels)


def from_padded(rows):
    channels = rows.shape[-1]
    split = rows.reshape(-1, GRID // WIN, SIDE, SIDE, channels)[:, :, :WIN, :WIN]
    return split.transpose(0, 2, 1, 3, 4).reshape(-1, WIN, GRID, channels)


def layernorm_apply(values, gain_vector, offset_vector):
    average = jnp.mean(values, axis=-1, keepdims=True)
    centered_input = values - average
    variance = jnp.mean(centered_input * centered_input, axis=-1, keepdims=True)
    inverse_deviation = lax.rsqrt(variance + EPS)
    standardized = centered_input * inverse_deviation
    return (standardized * gain_vector + offset_vector, standardized, inverse_deviation)


def layernorm_reverse(output_gradient, standardized, inverse_deviation, gain_vector):
    standardized_gradient = output_gradient * gain_vector
    input_gradient_rows = inverse_deviation * (
        standardized_gradient
        - jnp.mean(standardized_gradient, axis=-1, keepdims=True)
        - standardized * jnp.mean(standardized_gradient * standardized, axis=-1, keepdims=True)
    )
    return (
        input_gradient_rows,
        token_total(output_gradient * standardized),
        token_total(output_gradient),
    )


def gelu_value(preactivation):
    return preactivation * 0.5 * (1.0 + lax.erf(preactivation * SQRT_HALF))


def gelu_slope(preactivation):
    return (
        0.5 * (1.0 + lax.erf(preactivation * SQRT_HALF))
        + preactivation * jnp.exp(-0.5 * preactivation * preactivation) * INV_ROOT_TAU
    )


def head_lanes(dtype):
    shape = (GROUP, 1, LANES)
    head = lax.broadcasted_iota(jnp.int32, shape, 0)
    lane = lax.broadcasted_iota(jnp.int32, shape, 2)
    return (lane // HEAD_DIM == head).astype(jnp.float32).astype(dtype)


def spread(rows, lanes):
    return (rows[None] * lanes).reshape(GROUP * PAD, LANES)


def gather_heads(wide, lanes):
    return jnp.sum(wide.reshape(GROUP, PAD, LANES) * lanes, axis=0)


def dot_nt(left, right):
    return lax.dot_general(left, right, (((1,), (1,)), ((), ())), preferred_element_type=jnp.float32)


def dot_tn(left, right):
    return lax.dot_general(left, right, (((0,), (0,)), ((), ())), preferred_element_type=jnp.float32)


def window_probs(wide_query, keys, scores_bias):
    scores = dot_nt(wide_query, keys) + scores_bias
    weights = jnp.exp(scores - jnp.max(scores, axis=-1, keepdims=True))
    return weights / jnp.sum(weights, axis=-1, keepdims=True)


def attend_kernel(kinds, x_ref, w_ref, b_ref, sb_ref, packed_ref, context_ref):
    packed = jnp.dot(x_ref[...], w_ref[:, : 3 * C], preferred_element_type=jnp.float32)
    bias = b_ref[...]
    packed_ref[:, :C] = ((packed[:, :C] + bias[:, :C]) * HEAD_DIM ** (-0.5)).astype(jnp.bfloat16)
    packed_ref[:, C : 2 * C] = packed[:, C : 2 * C].astype(jnp.bfloat16)
    packed_ref[:, 2 * C :] = (packed[:, 2 * C :] + bias[:, C:]).astype(jnp.bfloat16)
    lanes = head_lanes(jnp.bfloat16)
    lanes_f32 = head_lanes(jnp.float32)

    def window(step, carry):
        rows = pl.ds(pl.multiple_of(step * PAD, PAD), PAD)
        kind = lax.rem(step, kinds)
        for group in range(GROUPS):
            low = group * LANES
            wide_query = spread(packed_ref[rows, low : low + LANES], lanes)
            keys = packed_ref[rows, C + low : C + low + LANES]
            values = packed_ref[rows, 2 * C + low : 2 * C + low + LANES]
            probs = window_probs(wide_query, keys, sb_ref[kind, group])
            wide = jnp.dot(
                probs.astype(jnp.bfloat16), values, preferred_element_type=jnp.float32
            )
            context_ref[rows, low : low + LANES] = gather_heads(wide, lanes_f32).astype(
                jnp.bfloat16
            )
        return carry

    lax.fori_loop(0, x_ref.shape[0] // PAD, window, 0)


def attend_back_kernel(kinds, packed_ref, dc_ref, sb_ref, dp_ref, db_ref, table_ref):
    lanes = head_lanes(jnp.bfloat16)
    lanes_f32 = head_lanes(jnp.float32)
    db_ref[...] = jnp.zeros_like(db_ref)
    table_ref[...] = jnp.zeros_like(table_ref)
    scale = HEAD_DIM ** (-0.5)

    def window(step, carry):
        rows = pl.ds(pl.multiple_of(step * PAD, PAD), PAD)
        kind = lax.rem(step, kinds)
        for group in range(GROUPS):
            low = group * LANES
            wide_query = spread(packed_ref[rows, low : low + LANES], lanes)
            keys = packed_ref[rows, C + low : C + low + LANES]
            values = packed_ref[rows, 2 * C + low : 2 * C + low + LANES]
            probs = window_probs(wide_query, keys, sb_ref[kind, group])
            wide_grad = spread(dc_ref[rows, low : low + LANES], lanes)
            grad_probs = dot_nt(wide_grad, values)
            grad_values = dot_tn(probs.astype(jnp.bfloat16), wide_grad)
            grad_scores = probs * (
                grad_probs - jnp.sum(probs * grad_probs, axis=-1, keepdims=True)
            )
            table_ref[group] += grad_scores
            scores_bf = grad_scores.astype(jnp.bfloat16)
            wide = jnp.dot(scores_bf, keys, preferred_element_type=jnp.float32)
            grad_query = gather_heads(wide, lanes_f32) * scale
            grad_keys = dot_tn(scores_bf, wide_query)
            dp_ref[rows, low : low + LANES] = grad_query.astype(jnp.bfloat16)
            dp_ref[rows, C + low : C + low + LANES] = grad_keys.astype(jnp.bfloat16)
            dp_ref[rows, 2 * C + low : 2 * C + low + LANES] = grad_values.astype(jnp.bfloat16)
            db_ref[:, low : low + LANES] += jnp.sum(grad_query, axis=0, keepdims=True)
            db_ref[:, C + low : C + low + LANES] += jnp.sum(grad_values, axis=0, keepdims=True)
        return carry

    lax.fori_loop(0, dc_ref.shape[0] // PAD, window, 0)


def in_vmem(count):
    return [pl.BlockSpec(memory_space=pltpu.VMEM)] * count


def attend(window_input, in_out_weight, in_bias, scores_bias):
    tokens = window_input.shape[0]
    kinds = scores_bias.shape[0]
    return pl.pallas_call(
        lambda *refs: attend_kernel(kinds, *refs),
        out_shape=(
            jax.ShapeDtypeStruct((tokens, 3 * C), jnp.bfloat16),
            jax.ShapeDtypeStruct((tokens, C), jnp.bfloat16),
        ),
        in_specs=in_vmem(4),
        out_specs=tuple(in_vmem(2)),
        cost_estimate=pl.CostEstimate(
            flops=8 * tokens * C * C, bytes_accessed=20 * 2**20, transcendentals=0
        ),
    )(window_input, in_out_weight, in_bias[None], scores_bias)


def attend_back(packed, grad_context, scores_bias):
    tokens = packed.shape[0]
    kinds = scores_bias.shape[0]
    return pl.pallas_call(
        lambda *refs: attend_back_kernel(kinds, *refs),
        out_shape=(
            jax.ShapeDtypeStruct((tokens, 3 * C), jnp.bfloat16),
            jax.ShapeDtypeStruct((1, 2 * C), jnp.float32),
            jax.ShapeDtypeStruct((GROUPS, GROUP * PAD, PAD), jnp.float32),
        ),
        in_specs=in_vmem(3),
        out_specs=tuple(in_vmem(3)),
        cost_estimate=pl.CostEstimate(
            flops=8 * tokens * C * C, bytes_accessed=40 * 2**20, transcendentals=0
        ),
    )(packed, grad_context, scores_bias)


def enter_grid(rows, shifted):
    if not shifted:
        return rows
    grid = from_padded(rows)
    incoming = swapped(grid[:, :SHIFT], "rows", 0)
    grid = jnp.concatenate([grid[:, SHIFT:], incoming], axis=1)
    return to_padded(jnp.roll(grid, -SHIFT, axis=2))


def leave_grid(rows, shifted):
    if not shifted:
        return rows
    grid = jnp.roll(from_padded(rows), SHIFT, axis=2)
    incoming = swapped(grid[:, WIN - SHIFT :].astype(jnp.bfloat16), "rows", 0).astype(grid.dtype)
    return to_padded(jnp.concatenate([incoming, grid[:, : WIN - SHIFT]], axis=1))


def layer_forward(stream, weights, vectors, scores_bias, shifted):
    in_out_weight, up_weight, down_weight = weights
    first_gain, first_offset, in_bias, out_bias = vectors[:4]
    second_gain, second_offset, up_bias, down_bias = vectors[4:]
    normalized, first_standardized, first_scale = layernorm_apply(stream, first_gain, first_offset)
    window_input = enter_grid(normalized.astype(jnp.bfloat16), shifted)
    packed, context = attend(window_input, in_out_weight, in_bias, scores_bias)
    local_context = leave_grid(context, shifted)
    attended = (
        stream
        + jnp.dot(local_context, in_out_weight[:, 3 * C :], preferred_element_type=jnp.float32)
        + out_bias
    )
    second_normalized, second_standardized, second_scale = layernorm_apply(
        attended, second_gain, second_offset
    )
    hidden = second_normalized.astype(jnp.bfloat16)
    preactivation = jnp.dot(hidden, up_weight, preferred_element_type=jnp.float32) + up_bias
    activated = gelu_value(preactivation).astype(jnp.bfloat16)
    result = (
        attended + jnp.dot(activated, down_weight, preferred_element_type=jnp.float32) + down_bias
    )
    kept = (
        first_standardized,
        first_scale,
        window_input,
        packed,
        local_context,
        second_standardized,
        second_scale,
        hidden,
        preactivation,
        activated,
    )
    return result, kept


def layer_backward(grad_flow, weights, vectors, scores_bias, onehot, shifted, kept):
    in_out_weight, up_weight, down_weight = weights
    first_gain, second_gain = vectors[0], vectors[4]
    (
        first_standardized,
        first_scale,
        window_input,
        packed,
        local_context,
        second_standardized,
        second_scale,
        hidden,
        preactivation,
        activated,
    ) = kept
    grad_bf = grad_flow.astype(jnp.bfloat16)
    grad_down = outer(activated, grad_bf)
    grad_down_bias = token_total(grad_flow)
    grad_pre = back_product(grad_bf, down_weight) * gelu_slope(preactivation)
    grad_pre_bf = grad_pre.astype(jnp.bfloat16)
    grad_up = outer(hidden, grad_pre_bf)
    grad_up_bias = token_total(grad_pre)
    attention_share, second_gain_gradient, second_offset_gradient = layernorm_reverse(
        back_product(grad_pre_bf, up_weight), second_standardized, second_scale, second_gain
    )
    mlp_shards = scatter_sum(owner_blocks((grad_up, grad_down)))
    grad_mixed = grad_flow + attention_share
    mixed_bf = grad_mixed.astype(jnp.bfloat16)
    grad_out = outer(local_context, mixed_bf)
    grad_out_bias = token_total(grad_mixed)
    grad_context = back_product(mixed_bf, in_out_weight[:, 3 * C :]).astype(jnp.bfloat16)
    grad_packed, grad_in_bias, table_term = attend_back(
        packed, enter_grid(grad_context, shifted), scores_bias
    )
    grad_in = outer(window_input, grad_packed)
    attn_shards = scatter_sum(owner_blocks((grad_in, grad_out)))
    normalized_gradient = leave_grid(
        back_product(grad_packed, in_out_weight[:, : 3 * C]), shifted
    )
    residual_share, first_gain_gradient, first_offset_gradient = layernorm_reverse(
        normalized_gradient, first_standardized, first_scale, first_gain
    )
    grad_table = lax.dot_general(
        onehot,
        table_term.reshape(HEADS, -1),
        (((0,), (1,)), ((), ())),
        precision=lax.Precision.HIGHEST,
    )
    vector_grads = (
        first_gain_gradient,
        first_offset_gradient,
        grad_in_bias.reshape(-1),
        grad_out_bias,
        second_gain_gradient,
        second_offset_gradient,
        grad_up_bias,
        grad_down_bias,
    )
    return grad_mixed + residual_share, mlp_shards, attn_shards, vector_grads, grad_table


def owner_blocks(grads):
    owners = lax.axis_size("dp")
    parts = []
    for grad in grads:
        depth = grad.shape[0] // owners
        blocks = grad.astype(jnp.bfloat16).reshape(owners, depth, -1, C).transpose(0, 2, 1, 3)
        parts.append(blocks.reshape(owners, -1, C))
    return jnp.concatenate(parts, axis=1)


def from_blocks(block, depth):
    return block.reshape(-1, depth, C).transpose(1, 0, 2).reshape(depth, -1)


def halve(array, axis_name, bit, dim):
    mine = (lax.axis_index(axis_name) >> bit) & 1
    keep = lax.dynamic_index_in_dim(array, mine, dim, keepdims=False)
    away = lax.dynamic_index_in_dim(array, 1 - mine, dim, keepdims=False)
    return add_bf(keep, swapped(away, axis_name, bit))


def add_bf(left, right):
    return (left.astype(jnp.float32) + right.astype(jnp.float32)).astype(jnp.bfloat16)


def halve_owner(blocks, bit):
    owners, rows, _ = blocks.shape
    return halve(blocks.reshape(owners // 2, 2, rows, C), "dp", bit, 1)


def halve_rows(blocks):
    owners, rows, _ = blocks.shape
    return halve(blocks.reshape(owners, 2, rows // 2, C), "rows", 0, 1)


def scatter_sum(blocks):
    bits = (lax.axis_size("dp") - 1).bit_length()
    blocks = halve_owner(blocks, 0)
    half = blocks.shape[1] // 2
    first, second = blocks[:, :half], blocks[:, half:]
    first, second = halve_owner(first, 1), halve_rows(second)
    first, second = halve_rows(first), halve_owner(second, 1)
    both = jnp.concatenate([first, second], axis=1)
    for bit in range(2, bits):
        both = halve_owner(both, bit)
    both = both[0].reshape(2, -1, C)
    other = swapped(both, "rows", 0)
    upper = lax.axis_index("rows") == 1
    low, high = jnp.where(upper, other, both), jnp.where(upper, both, other)
    return jnp.stack([low, high], axis=1).reshape(-1, C).astype(jnp.float32)


def gathered(piece):
    return lax.all_gather(piece, "dp", axis=0, tiled=True)


def per_device(
    images,
    cotangent,
    attn_in_weight,
    attn_out_weight,
    mlp_in_weight,
    mlp_out_weight,
    norm1_gain,
    norm1_bias,
    attn_in_bias,
    attn_out_bias,
    norm2_gain,
    norm2_bias,
    mlp_in_bias,
    mlp_out_bias,
    bias_table,
    region_labels,
    table_index,
):
    owners = lax.axis_size("dp")
    vector_shards = (
        norm1_gain,
        norm1_bias,
        attn_in_bias,
        attn_out_bias,
        norm2_gain,
        norm2_bias,
        mlp_in_bias,
        mlp_out_bias,
    )
    widths = [member.shape[1] for member in vector_shards]
    vector_all = gathered(jnp.concatenate(vector_shards, axis=1).reshape(1, -1))
    vector_all = vector_all.reshape(owners, LAYERS, -1).astype(jnp.float32)

    def layer_vectors(layer_no):
        start, result = 0, []
        for width in widths:
            result.append(vector_all[:, layer_no, start : start + width].reshape(-1))
            start += width
        return tuple(result)

    def layer_weights(layer_no):
        in_out = jnp.concatenate([attn_in_weight[layer_no], attn_out_weight[layer_no]], axis=1)
        return gathered(in_out), gathered(mlp_in_weight[layer_no]), gathered(mlp_out_weight[layer_no])

    def pad_window(values, fill):
        grid = values.reshape(values.shape[:-1] + (WIN, WIN))
        pads = [(0, 0)] * (values.ndim - 1) + [(0, SIDE - WIN)] * 2
        return jnp.pad(grid, pads, constant_values=fill).reshape(values.shape[:-1] + (PAD,))

    def pad_pair(values, fill):
        both = pad_window(jnp.swapaxes(pad_window(values, fill), -1, -2), fill)
        return jnp.swapaxes(both, -1, -2)

    half_index = lax.axis_index("rows")
    local_labels = lax.dynamic_slice_in_dim(region_labels, half_index * WIN, WIN, 0)
    label_tiles = (
        local_labels.reshape(WIN, GRID // WIN, WIN).transpose(1, 0, 2).reshape(GRID // WIN, -1)
    )
    same = label_tiles[:, :, None] == label_tiles[:, None, :]
    real_key = pad_window(jnp.ones((WIN * WIN,), jnp.int32), 0) == 1
    allowed_pair = (
        jnp.broadcast_to(real_key[None, None, :], (1, PAD, PAD)),
        (pad_pair(same.astype(jnp.int32), 1) == 1) & real_key[None, None, :],
    )
    index_pad = pad_pair(table_index, 0)
    onehot = (index_pad.reshape(-1)[:, None] == jnp.arange(REL, dtype=jnp.int32)[None, :]).astype(
        jnp.float32
    )

    def scores_bias_of(layer_no):
        picked = jnp.take(bias_table[layer_no], index_pad.reshape(-1), axis=0).T
        picked = picked.reshape(HEADS, PAD, PAD)
        allowed = allowed_pair[layer_no % 2]
        masked = jnp.where(allowed[:, None], picked[None], NEG)
        return masked.reshape(-1, GROUPS, GROUP * PAD, PAD)

    stream = to_padded(images).astype(jnp.float32)
    weights = [layer_weights(layer_no) for layer_no in range(LAYERS)]
    vectors = [layer_vectors(layer_no) for layer_no in range(LAYERS)]
    score_biases = [scores_bias_of(layer_no) for layer_no in range(LAYERS)]
    kept_all = []
    for layer_no in range(LAYERS):
        stream, kept = layer_forward(
            stream, weights[layer_no], vectors[layer_no], score_biases[layer_no], layer_no % 2 == 1
        )
        kept_all.append(kept)
    final_out = from_padded(stream.astype(jnp.bfloat16))
    grad_flow = to_padded(cotangent).astype(jnp.float32)
    mlp_all, attn_all, vectors_all, tables_all = ([None] * LAYERS for _ in range(4))
    for layer_no in reversed(range(LAYERS)):
        grad_flow, mlp_all[layer_no], attn_all[layer_no], grads, tables_all[layer_no] = (
            layer_backward(
                grad_flow,
                weights[layer_no],
                vectors[layer_no],
                score_biases[layer_no],
                onehot,
                layer_no % 2 == 1,
                kept_all[layer_no],
            )
        )
        vectors_all[layer_no] = jnp.concatenate(grads)
    lengths = [width * owners for width in widths]
    small = jnp.concatenate(vectors_all + [jnp.stack(tables_all).reshape(-1)])
    total = small.shape[0]
    small = jnp.pad(small, (0, -total % (8 * LANES))).reshape(-1, LANES)
    small = lax.psum(small, ("rows", "dp")).reshape(-1)[:total]
    vector_total = small[: LAYERS * sum(lengths)].reshape(LAYERS, -1)
    table_total = small[LAYERS * sum(lengths) :].reshape(bias_table.shape)
    vector_outs, start = [], 0
    owner = lax.axis_index("dp")
    for width, length in zip(widths, lengths):
        part = vector_total[:, start : start + length]
        vector_outs.append(lax.dynamic_slice_in_dim(part, owner * width, width, 1))
        start += length
    depth = attn_in_weight.shape[1]

    def stacked(blocks, low, high, rows):
        return jnp.stack([from_blocks(block[low * depth : high * depth], rows) for block in blocks])

    down_depth = mlp_out_weight.shape[1]
    up_blocks = mlp_in_weight.shape[2] // C
    grad_up = stacked(mlp_all, 0, up_blocks, depth)
    grad_down = jnp.stack([block[up_blocks * depth :].reshape(down_depth, C) for block in mlp_all])
    grad_in = stacked(attn_all, 0, 3, depth)
    grad_out = stacked(attn_all, 3, 4, depth)
    return (
        final_out,
        from_padded(grad_flow),
        grad_in,
        grad_out,
        grad_up,
        grad_down,
        *vector_outs,
        table_total,
    )


def solution(mesh):
    return jax.shard_map(
        per_device,
        mesh=mesh,
        in_specs=(
            P("dp", "rows", None, None),
            P("dp", "rows", None, None),
            P(None, "dp", None),
            P(None, "dp", None),
            P(None, "dp", None),
            P(None, "dp", None),
            P(None, "dp"),
            P(None, "dp"),
            P(None, "dp"),
            P(None, "dp"),
            P(None, "dp"),
            P(None, "dp"),
            P(None, "dp"),
            P(None, "dp"),
            P(),
            P(),
            P(),
        ),
        out_specs=(
            P("dp", "rows", None, None),
            P("dp", "rows", None, None),
            P(None, "dp", None),
            P(None, "dp", None),
            P(None, "dp", None),
            P(None, "dp", None),
            P(None, "dp"),
            P(None, "dp"),
            P(None, "dp"),
            P(None, "dp"),
            P(None, "dp"),
            P(None, "dp"),
            P(None, "dp"),
            P(None, "dp"),
            P(),
        ),
        check_vma=False,
    )
```

```python
import jax
import jax.numpy as jnp
from jax import lax
from jax.experimental import pallas as pl
from jax.experimental.pallas import tpu as pltpu
from jax.sharding import PartitionSpec as P

C = 512
HEADS = 16
HEAD_DIM = 32
WIN = 7
GRID = 14
SHIFT = 3
LAYERS = 2
REL = 169
SIDE = 8
PAD = SIDE * SIDE
LANES = 128
GROUP = LANES // HEAD_DIM
GROUPS = HEADS // GROUP


EPS = 1e-05
NEG = -1e30
SQRT_HALF = 0.7071067811865476
INV_ROOT_TAU = 0.3989422804014327


def swapped(array, axis, distance):
    return lax.ppermute(array, axis, [(i, i ^ 1 << distance) for i in range(lax.axis_size(axis))])


def product(spec, left, right):
    return jnp.einsum(spec, left, right, preferred_element_type=jnp.float32)


def outer(left, right):
    left_flat = left.reshape(-1, left.shape[-1])
    right_flat = right.reshape(-1, right.shape[-1])
    return lax.dot_general(
        left_flat, right_flat, (((0,), (0,)), ((), ())), preferred_element_type=jnp.float32
    )


def back_product(grad_rows, weight):
    return lax.dot_general(
        grad_rows,
        weight,
        (((grad_rows.ndim - 1,), (1,)), ((), ())),
        preferred_element_type=jnp.float32,
    )


def token_total(values):
    return jnp.sum(values.reshape(-1, values.shape[-1]), axis=0)


def to_padded(grid):
    images, _, cols, channels = grid.shape
    split = grid.reshape(images, WIN, cols // WIN, WIN, channels).transpose(0, 2, 1, 3, 4)
    padded = jnp.pad(split, ((0, 0), (0, 0), (0, SIDE - WIN), (0, SIDE - WIN), (0, 0)))
    return padded.reshape(-1, channels)


def from_padded(rows):
    channels = rows.shape[-1]
    split = rows.reshape(-1, GRID // WIN, SIDE, SIDE, channels)[:, :, :WIN, :WIN]
    return split.transpose(0, 2, 1, 3, 4).reshape(-1, WIN, GRID, channels)


def layernorm_apply(values, gain_vector, offset_vector):
    average = jnp.mean(values, axis=-1, keepdims=True)
    centered_input = values - average
    variance = jnp.mean(centered_input * centered_input, axis=-1, keepdims=True)
    inverse_deviation = lax.rsqrt(variance + EPS)
    standardized = centered_input * inverse_deviation
    return (standardized * gain_vector + offset_vector, standardized, inverse_deviation)


def layernorm_reverse(output_gradient, standardized, inverse_deviation, gain_vector):
    standardized_gradient = output_gradient * gain_vector
    input_gradient_rows = inverse_deviation * (
        standardized_gradient
        - jnp.mean(standardized_gradient, axis=-1, keepdims=True)
        - standardized * jnp.mean(standardized_gradient * standardized, axis=-1, keepdims=True)
    )
    return (
        input_gradient_rows,
        token_total(output_gradient * standardized),
        token_total(output_gradient),
    )


def gelu_value(preactivation):
    return preactivation * 0.5 * (1.0 + lax.erf(preactivation * SQRT_HALF))


def gelu_slope(preactivation):
    return (
        0.5 * (1.0 + lax.erf(preactivation * SQRT_HALF))
        + preactivation * jnp.exp(-0.5 * preactivation * preactivation) * INV_ROOT_TAU
    )


def head_lanes(dtype):
    shape = (GROUP, 1, LANES)
    head = lax.broadcasted_iota(jnp.int32, shape, 0)
    lane = lax.broadcasted_iota(jnp.int32, shape, 2)
    return (lane // HEAD_DIM == head).astype(jnp.float32).astype(dtype)


def spread(rows, lanes):
    return (rows[None] * lanes).reshape(GROUP * PAD, LANES)


def gather_heads(wide, lanes):
    return jnp.sum(wide.reshape(GROUP, PAD, LANES) * lanes, axis=0)


def dot_nt(left, right):
    return lax.dot_general(left, right, (((1,), (1,)), ((), ())), preferred_element_type=jnp.float32)


def dot_tn(left, right):
    return lax.dot_general(left, right, (((0,), (0,)), ((), ())), preferred_element_type=jnp.float32)


def window_probs(wide_query, keys, scores_bias):
    scores = dot_nt(wide_query, keys) + scores_bias
    weights = jnp.exp(scores - jnp.max(scores, axis=-1, keepdims=True))
    return weights / jnp.sum(weights, axis=-1, keepdims=True)


def attend_kernel(kinds, x_ref, w_ref, b_ref, sb_ref, packed_ref, context_ref):
    rows = x_ref[...]
    bias = b_ref[...]
    queries = jnp.dot(rows, w_ref[:, :C], preferred_element_type=jnp.float32) + bias[:, :C]
    packed_ref[:, :C] = (queries * HEAD_DIM ** (-0.5)).astype(jnp.bfloat16)
    keys = jnp.dot(rows, w_ref[:, C : 2 * C], preferred_element_type=jnp.float32)
    packed_ref[:, C : 2 * C] = keys.astype(jnp.bfloat16)
    values = jnp.dot(rows, w_ref[:, 2 * C :], preferred_element_type=jnp.float32) + bias[:, C:]
    packed_ref[:, 2 * C :] = values.astype(jnp.bfloat16)
    lanes = head_lanes(jnp.bfloat16)
    lanes_f32 = head_lanes(jnp.float32)

    def window(step, carry):
        rows = pl.ds(pl.multiple_of(step * PAD, PAD), PAD)
        kind = lax.rem(step, kinds)
        for group in range(GROUPS):
            low = group * LANES
            wide_query = spread(packed_ref[rows, low : low + LANES], lanes)
            keys = packed_ref[rows, C + low : C + low + LANES]
            values = packed_ref[rows, 2 * C + low : 2 * C + low + LANES]
            probs = window_probs(wide_query, keys, sb_ref[kind, group])
            wide = jnp.dot(
                probs.astype(jnp.bfloat16), values, preferred_element_type=jnp.float32
            )
            context_ref[rows, low : low + LANES] = gather_heads(wide, lanes_f32).astype(
                jnp.bfloat16
            )
        return carry

    lax.fori_loop(0, x_ref.shape[0] // PAD, window, 0)


def attend_back_kernel(kinds, packed_ref, dc_ref, sb_ref, dp_ref, db_ref, table_ref):
    lanes = head_lanes(jnp.bfloat16)
    lanes_f32 = head_lanes(jnp.float32)
    db_ref[...] = jnp.zeros_like(db_ref)
    table_ref[...] = jnp.zeros_like(table_ref)
    scale = HEAD_DIM ** (-0.5)

    def window(step, carry):
        rows = pl.ds(pl.multiple_of(step * PAD, PAD), PAD)
        kind = lax.rem(step, kinds)
        for group in range(GROUPS):
            low = group * LANES
            wide_query = spread(packed_ref[rows, low : low + LANES], lanes)
            keys = packed_ref[rows, C + low : C + low + LANES]
            values = packed_ref[rows, 2 * C + low : 2 * C + low + LANES]
            probs = window_probs(wide_query, keys, sb_ref[kind, group])
            wide_grad = spread(dc_ref[rows, low : low + LANES], lanes)
            grad_probs = dot_nt(wide_grad, values)
            grad_values = dot_tn(probs.astype(jnp.bfloat16), wide_grad)
            grad_scores = probs * (
                grad_probs - jnp.sum(probs * grad_probs, axis=-1, keepdims=True)
            )
            table_ref[group] += grad_scores
            scores_bf = grad_scores.astype(jnp.bfloat16)
            wide = jnp.dot(scores_bf, keys, preferred_element_type=jnp.float32)
            grad_query = gather_heads(wide, lanes_f32) * scale
            grad_keys = dot_tn(scores_bf, wide_query)
            dp_ref[rows, low : low + LANES] = grad_query.astype(jnp.bfloat16)
            dp_ref[rows, C + low : C + low + LANES] = grad_keys.astype(jnp.bfloat16)
            dp_ref[rows, 2 * C + low : 2 * C + low + LANES] = grad_values.astype(jnp.bfloat16)
            db_ref[:, low : low + LANES] += jnp.sum(grad_query, axis=0, keepdims=True)
            db_ref[:, C + low : C + low + LANES] += jnp.sum(grad_values, axis=0, keepdims=True)
        return carry

    lax.fori_loop(0, dc_ref.shape[0] // PAD, window, 0)


def in_vmem(count):
    return [pl.BlockSpec(memory_space=pltpu.VMEM)] * count


def attend(window_input, in_weight, in_bias, scores_bias):
    tokens = window_input.shape[0]
    kinds = scores_bias.shape[0]
    return pl.pallas_call(
        lambda *refs: attend_kernel(kinds, *refs),
        out_shape=(
            jax.ShapeDtypeStruct((tokens, 3 * C), jnp.bfloat16),
            jax.ShapeDtypeStruct((tokens, C), jnp.bfloat16),
        ),
        in_specs=in_vmem(4),
        out_specs=tuple(in_vmem(2)),
        cost_estimate=pl.CostEstimate(
            flops=8 * tokens * C * C, bytes_accessed=20 * 2**20, transcendentals=0
        ),
    )(window_input, in_weight, in_bias[None], scores_bias)


def attend_back(packed, grad_context, scores_bias):
    tokens = packed.shape[0]
    kinds = scores_bias.shape[0]
    return pl.pallas_call(
        lambda *refs: attend_back_kernel(kinds, *refs),
        out_shape=(
            jax.ShapeDtypeStruct((tokens, 3 * C), jnp.bfloat16),
            jax.ShapeDtypeStruct((1, 2 * C), jnp.float32),
            jax.ShapeDtypeStruct((GROUPS, GROUP * PAD, PAD), jnp.float32),
        ),
        in_specs=in_vmem(3),
        out_specs=tuple(in_vmem(3)),
        cost_estimate=pl.CostEstimate(
            flops=8 * tokens * C * C, bytes_accessed=40 * 2**20, transcendentals=0
        ),
    )(packed, grad_context, scores_bias)


def enter_grid(rows, shifted):
    if not shifted:
        return rows
    grid = from_padded(rows)
    incoming = swapped(grid[:, :SHIFT], "rows", 0)
    grid = jnp.concatenate([grid[:, SHIFT:], incoming], axis=1)
    return to_padded(jnp.roll(grid, -SHIFT, axis=2))


def leave_grid(rows, shifted):
    if not shifted:
        return rows
    grid = jnp.roll(from_padded(rows), SHIFT, axis=2)
    incoming = swapped(grid[:, WIN - SHIFT :].astype(jnp.bfloat16), "rows", 0).astype(grid.dtype)
    return to_padded(jnp.concatenate([incoming, grid[:, : WIN - SHIFT]], axis=1))


def layer_forward(stream, attn_weights, take_mlp, vectors, scores_bias, shifted, weave):
    in_weight, out_weight = attn_weights
    first_gain, first_offset, in_bias, out_bias = vectors[:4]
    second_gain, second_offset, up_bias, down_bias = vectors[4:]
    normalized, first_standardized, first_scale = layernorm_apply(stream, first_gain, first_offset)
    window_input = enter_grid(weave(normalized.astype(jnp.bfloat16)), shifted)
    window_input = weave(window_input)
    packed, context = attend(window_input, in_weight, in_bias, scores_bias)
    local_context = weave(leave_grid(weave(context), shifted))
    attended = (
        stream
        + jnp.dot(local_context, out_weight, preferred_element_type=jnp.float32)
        + out_bias
    )
    second_normalized, second_standardized, second_scale = layernorm_apply(
        attended, second_gain, second_offset
    )
    hidden = weave(second_normalized.astype(jnp.bfloat16))
    up_weight, down_weight = take_mlp()
    preactivation = jnp.dot(hidden, up_weight, preferred_element_type=jnp.float32) + up_bias
    activated = weave(gelu_value(preactivation).astype(jnp.bfloat16))
    result = (
        attended + jnp.dot(activated, down_weight, preferred_element_type=jnp.float32) + down_bias
    )
    kept = (
        first_standardized,
        first_scale,
        window_input,
        packed,
        local_context,
        second_standardized,
        second_scale,
        hidden,
        preactivation,
        activated,
    )
    return result, kept


def layer_backward(
    grad_flow, weights, vectors, scores_bias, onehot, shifted, kept, weave
):
    in_weight, out_weight, up_weight, down_weight = weights
    first_gain, second_gain = vectors[0], vectors[4]
    (
        first_standardized,
        first_scale,
        window_input,
        packed,
        local_context,
        second_standardized,
        second_scale,
        hidden,
        preactivation,
        activated,
    ) = kept
    grad_bf = grad_flow.astype(jnp.bfloat16)
    grad_down = outer(activated, grad_bf)
    grad_down_bias = token_total(grad_flow)
    grad_pre = back_product(grad_bf, down_weight) * gelu_slope(preactivation)
    grad_pre_bf = weave(grad_pre.astype(jnp.bfloat16))
    grad_up = outer(hidden, grad_pre_bf)
    grad_up_bias = token_total(grad_pre)
    attention_share, second_gain_gradient, second_offset_gradient = layernorm_reverse(
        back_product(grad_pre_bf, up_weight), second_standardized, second_scale, second_gain
    )
    attention_share = weave(attention_share)
    mlp_shards = weave.add(scatter_steps(owner_blocks((grad_up, grad_down))))
    grad_mixed = grad_flow + attention_share
    mixed_bf = grad_mixed.astype(jnp.bfloat16)
    grad_out = outer(local_context, mixed_bf)
    grad_out_bias = token_total(grad_mixed)
    grad_context = weave(back_product(mixed_bf, out_weight).astype(jnp.bfloat16))
    grad_packed, grad_in_bias, table_term = attend_back(
        packed, weave(enter_grid(grad_context, shifted)), scores_bias
    )
    grad_packed = weave(grad_packed)
    grad_in = outer(window_input, grad_packed)
    attn_shards = weave.add(scatter_steps(owner_blocks((grad_in, grad_out))))
    normalized_gradient = weave(leave_grid(weave(back_product(grad_packed, in_weight)), shifted))
    residual_share, first_gain_gradient, first_offset_gradient = layernorm_reverse(
        normalized_gradient, first_standardized, first_scale, first_gain
    )
    grad_table = lax.dot_general(
        onehot,
        table_term.reshape(HEADS, -1),
        (((0,), (1,)), ((), ())),
        precision=lax.Precision.HIGHEST,
    )
    vector_grads = (
        first_gain_gradient,
        first_offset_gradient,
        grad_in_bias.reshape(-1),
        grad_out_bias,
        second_gain_gradient,
        second_offset_gradient,
        grad_up_bias,
        grad_down_bias,
    )
    return grad_mixed + residual_share, mlp_shards, attn_shards, vector_grads, grad_table


class Chain:
    def __init__(self, steps):
        self.steps = steps
        self.state = next(steps)
        self.done = False

    def advance(self):
        following = next(self.steps, None)
        if following is None:
            self.done = True
        else:
            self.state = following

    def finish(self):
        while not self.done:
            self.advance()
        return self.state


class Weave:
    def __init__(self):
        self.chains = []

    def add(self, steps):
        chain = Chain(steps)
        self.chains.append(chain)
        return chain

    def __call__(self, value):
        live = [chain for chain in self.chains if not chain.done]
        for chain in live:
            chain.advance()
        if live:
            value, states = lax.optimization_barrier((value, [chain.state for chain in live]))
            for chain, state in zip(live, states):
                chain.state = state
        return value


def owner_blocks(grads):
    owners = lax.axis_size("dp")
    parts = []
    for grad in grads:
        grad = grad.astype(jnp.bfloat16)
        for low in range(0, grad.shape[1], C):
            parts.append(grad[:, low : low + C].reshape(owners, -1, C))
    return jnp.concatenate(parts, axis=1)


def merge(array, axis_name, bit):
    other = swapped(array, axis_name, bit)
    upper = ((lax.axis_index(axis_name) >> bit) & 1) == 1
    return jnp.where(upper, other, array), jnp.where(upper, array, other)


def double_owner(blocks, bit):
    owners, rows, _ = blocks.shape
    return jnp.stack(merge(blocks, "dp", bit), axis=1).reshape(2 * owners, rows, C)


def double_rows(blocks):
    return jnp.concatenate(merge(blocks, "rows", 0), axis=1)


def gather_steps(piece):
    bits = (lax.axis_size("dp") - 1).bit_length()
    quarters = piece.reshape(2, 2, -1, C)
    blocks = lax.dynamic_index_in_dim(quarters, lax.axis_index("rows"), 1, keepdims=False)
    blocks = blocks.reshape(1, -1, C)
    yield blocks
    for bit in range(bits - 1, 1, -1):
        blocks = double_owner(blocks, bit)
        yield blocks
    half = blocks.shape[1] // 2
    first, second = blocks[:, :half], blocks[:, half:]
    first, second = double_owner(first, 1), double_rows(second)
    yield first, second
    blocks = jnp.concatenate([double_rows(first), double_owner(second, 1)], axis=1)
    yield blocks
    yield double_owner(blocks, 0)


def piece_blocks(pieces):
    parts = []
    for piece in pieces:
        parts.extend(piece[:, low : low + C] for low in range(0, piece.shape[1], C))
    return jnp.concatenate(parts, axis=0)


def columns_of(blocks, count):
    depth = blocks.shape[1] // count
    parts = [
        blocks[:, step * depth : (step + 1) * depth].reshape(-1, C) for step in range(count)
    ]
    return jnp.concatenate(parts, axis=1)


def all_sum(values):
    for axis_name in ("dp", "rows"):
        for bit in range((lax.axis_size(axis_name) - 1).bit_length()):
            values = values + swapped(values, axis_name, bit)
    return values


def from_blocks(block, depth):
    return block.reshape(-1, depth, C).transpose(1, 0, 2).reshape(depth, -1)


def halve(array, axis_name, bit, dim):
    mine = (lax.axis_index(axis_name) >> bit) & 1
    keep = lax.dynamic_index_in_dim(array, mine, dim, keepdims=False)
    away = lax.dynamic_index_in_dim(array, 1 - mine, dim, keepdims=False)
    return add_bf(keep, swapped(away, axis_name, bit))


def add_bf(left, right):
    return (left.astype(jnp.float32) + right.astype(jnp.float32)).astype(jnp.bfloat16)


def halve_owner(blocks, bit):
    owners, rows, _ = blocks.shape
    return halve(blocks.reshape(owners // 2, 2, rows, C), "dp", bit, 1)


def halve_rows(blocks):
    owners, rows, _ = blocks.shape
    return halve(blocks.reshape(owners, 2, rows // 2, C), "rows", 0, 1)


def scatter_steps(blocks):
    bits = (lax.axis_size("dp") - 1).bit_length()
    yield blocks
    blocks = halve_owner(blocks, 0)
    yield blocks
    half = blocks.shape[1] // 2
    first, second = blocks[:, :half], blocks[:, half:]
    first, second = halve_owner(first, 1), halve_rows(second)
    yield first, second
    first, second = halve_rows(first), halve_owner(second, 1)
    both = jnp.concatenate([first, second], axis=1)
    yield both
    for bit in range(2, bits):
        both = halve_owner(both, bit)
        yield both
    low, high = merge(both[0].reshape(2, -1, C), "rows", 0)
    yield jnp.stack([low, high], axis=1).reshape(-1, C).astype(jnp.float32)


def per_device(
    images,
    cotangent,
    attn_in_weight,
    attn_out_weight,
    mlp_in_weight,
    mlp_out_weight,
    norm1_gain,
    norm1_bias,
    attn_in_bias,
    attn_out_bias,
    norm2_gain,
    norm2_bias,
    mlp_in_bias,
    mlp_out_bias,
    bias_table,
    region_labels,
    table_index,
):
    owners = lax.axis_size("dp")
    vector_shards = (
        norm1_gain,
        norm1_bias,
        attn_in_bias,
        attn_out_bias,
        norm2_gain,
        norm2_bias,
        mlp_in_bias,
        mlp_out_bias,
    )
    widths = [member.shape[1] for member in vector_shards]
    vector_piece = jnp.concatenate(vector_shards, axis=1).reshape(-1)
    vector_size = vector_piece.shape[0]
    vector_piece = jnp.pad(vector_piece, (0, -vector_size % (32 * C))).reshape(-1, C)
    depth = attn_in_weight.shape[1]
    up_blocks = mlp_in_weight.shape[2] // C

    def attn_piece(layer_no):
        return piece_blocks([attn_in_weight[layer_no], attn_out_weight[layer_no]])

    def mlp_piece(layer_no):
        return piece_blocks([mlp_in_weight[layer_no], mlp_out_weight[layer_no]])

    def attn_split(blocks):
        blocks = blocks[:, : 4 * depth]
        return columns_of(blocks[:, : 3 * depth], 3), blocks[:, 3 * depth :].reshape(-1, C)

    def mlp_split(blocks):
        up, down = blocks[:, : up_blocks * depth], blocks[:, up_blocks * depth :]
        return columns_of(up, up_blocks), down.reshape(-1, C)

    lead = Chain(gather_steps(jnp.concatenate([attn_piece(0), vector_piece], axis=0)))
    lead.advance()
    lead.advance()
    lead.state, first_mlp = lax.optimization_barrier((lead.state, mlp_piece(0)))
    weave = Weave()
    mlp_chains = [weave.add(gather_steps(first_mlp))]
    lead.advance()
    lead.state = weave(lead.state)
    lead.advance()
    lead.state = weave(lead.state)
    lead_blocks = lead.finish()
    vector_all = lead_blocks[:, 4 * depth :].reshape(owners, -1)[:, :vector_size]
    vector_all = vector_all.reshape(owners, LAYERS, -1).astype(jnp.float32)

    def layer_vectors(layer_no):
        start, result = 0, []
        for width in widths:
            result.append(vector_all[:, layer_no, start : start + width].reshape(-1))
            start += width
        return tuple(result)

    def pad_window(values, fill):
        grid = values.reshape(values.shape[:-1] + (WIN, WIN))
        pads = [(0, 0)] * (values.ndim - 1) + [(0, SIDE - WIN)] * 2
        return jnp.pad(grid, pads, constant_values=fill).reshape(values.shape[:-1] + (PAD,))

    def pad_pair(values, fill):
        both = pad_window(jnp.swapaxes(pad_window(values, fill), -1, -2), fill)
        return jnp.swapaxes(both, -1, -2)

    half_index = lax.axis_index("rows")
    local_labels = lax.dynamic_slice_in_dim(region_labels, half_index * WIN, WIN, 0)
    label_tiles = (
        local_labels.reshape(WIN, GRID // WIN, WIN).transpose(1, 0, 2).reshape(GRID // WIN, -1)
    )
    same = label_tiles[:, :, None] == label_tiles[:, None, :]
    real_key = pad_window(jnp.ones((WIN * WIN,), jnp.int32), 0) == 1
    allowed_pair = (
        jnp.broadcast_to(real_key[None, None, :], (1, PAD, PAD)),
        (pad_pair(same.astype(jnp.int32), 1) == 1) & real_key[None, None, :],
    )
    index_pad = pad_pair(table_index, 0)
    onehot = (index_pad.reshape(-1)[:, None] == jnp.arange(REL, dtype=jnp.int32)[None, :]).astype(
        jnp.float32
    )

    def scores_bias_of(layer_no):
        picked = lax.dot_general(
            bias_table[layer_no],
            onehot,
            (((0,), (1,)), ((), ())),
            precision=lax.Precision.HIGHEST,
            preferred_element_type=jnp.float32,
        ).reshape(HEADS, PAD, PAD)
        allowed = allowed_pair[layer_no % 2]
        masked = jnp.where(allowed[:, None], picked[None], NEG)
        return masked.reshape(-1, GROUPS, GROUP * PAD, PAD)

    stream = to_padded(images).astype(jnp.float32)
    vectors = [layer_vectors(layer_no) for layer_no in range(LAYERS)]
    score_biases = [scores_bias_of(layer_no) for layer_no in range(LAYERS)]
    kept_all = []
    attn_chains = [lead]
    weights = []
    for layer_no in range(LAYERS):
        if layer_no + 1 < LAYERS:
            attn_chains.append(weave.add(gather_steps(attn_piece(layer_no + 1))))
        attn_weights = attn_split(attn_chains[layer_no].finish())
        taken = []

        def take_mlp():
            taken.extend(mlp_split(mlp_chains[layer_no].finish()))
            if layer_no + 1 < LAYERS:
                mlp_chains.append(weave.add(gather_steps(mlp_piece(layer_no + 1))))
            return taken

        stream, kept = layer_forward(
            stream,
            attn_weights,
            take_mlp,
            vectors[layer_no],
            score_biases[layer_no],
            layer_no % 2 == 1,
            weave,
        )
        weights.append((*attn_weights, *taken))
        kept_all.append(kept)
    final_out = from_padded(stream.astype(jnp.bfloat16))
    grad_flow = to_padded(cotangent).astype(jnp.float32)
    mlp_all, attn_all, vectors_all, tables_all = ([None] * LAYERS for _ in range(4))
    for layer_no in reversed(range(LAYERS)):
        grad_flow, mlp_all[layer_no], attn_all[layer_no], grads, tables_all[layer_no] = (
            layer_backward(
                grad_flow,
                weights[layer_no],
                vectors[layer_no],
                score_biases[layer_no],
                onehot,
                layer_no % 2 == 1,
                kept_all[layer_no],
                weave,
            )
        )
        vectors_all[layer_no] = jnp.concatenate(grads)
    lengths = [width * owners for width in widths]
    small = jnp.concatenate(vectors_all + [jnp.stack(tables_all).reshape(-1)])
    total = small.shape[0]
    small = jnp.pad(small, (0, -total % (8 * LANES))).reshape(-1, LANES)
    small = all_sum(small).reshape(-1)[:total]
    mlp_all = [chain.finish() for chain in mlp_all]
    attn_all = [chain.finish() for chain in attn_all]
    vector_total = small[: LAYERS * sum(lengths)].reshape(LAYERS, -1)
    table_total = small[LAYERS * sum(lengths) :].reshape(bias_table.shape)
    vector_outs, start = [], 0
    owner = lax.axis_index("dp")
    for width, length in zip(widths, lengths):
        part = vector_total[:, start : start + length]
        vector_outs.append(lax.dynamic_slice_in_dim(part, owner * width, width, 1))
        start += length
    def stacked(blocks, low, high, rows):
        return jnp.stack([from_blocks(block[low * depth : high * depth], rows) for block in blocks])

    down_depth = mlp_out_weight.shape[1]
    grad_up = stacked(mlp_all, 0, up_blocks, depth)
    grad_down = jnp.stack([block[up_blocks * depth :].reshape(down_depth, C) for block in mlp_all])
    grad_in = stacked(attn_all, 0, 3, depth)
    grad_out = stacked(attn_all, 3, 4, depth)
    return (
        final_out,
        from_padded(grad_flow),
        grad_in,
        grad_out,
        grad_up,
        grad_down,
        *vector_outs,
        table_total,
    )


def solution(mesh):
    return jax.shard_map(
        per_device,
        mesh=mesh,
        in_specs=(
            P("dp", "rows", None, None),
            P("dp", "rows", None, None),
            P(None, "dp", None),
            P(None, "dp", None),
            P(None, "dp", None),
            P(None, "dp", None),
            P(None, "dp"),
            P(None, "dp"),
            P(None, "dp"),
            P(None, "dp"),
            P(None, "dp"),
            P(None, "dp"),
            P(None, "dp"),
            P(None, "dp"),
            P(),
            P(),
            P(),
        ),
        out_specs=(
            P("dp", "rows", None, None),
            P("dp", "rows", None, None),
            P(None, "dp", None),
            P(None, "dp", None),
            P(None, "dp", None),
            P(None, "dp", None),
            P(None, "dp"),
            P(None, "dp"),
            P(None, "dp"),
            P(None, "dp"),
            P(None, "dp"),
            P(None, "dp"),
            P(None, "dp"),
            P(None, "dp"),
            P(),
        ),
        check_vma=False,
    )
```
